512 devices in a mesh: layer: 16 (over x, z_hi, core), col: 32 (over z_lo, y).
Axes of the slice: x: 4, y: 8, z: 8 (z_hi: 2, z_lo: 4; z = z_hi * 4 + z_lo), core: 2. Of those that a mesh axis runs over, the one named last changes fastest.
Arguments:
- lower_panel: bfloat16 [16, 4096, 768], P('layer', 'col'), may hold values from -0.109375 to 0.109375
- upper_panel: bfloat16 [16, 768, 4096], P('layer', None, 'col'), may hold values from -6 to 6
- diag_inverse: bfloat16 [16, 1, 768, 768], P('layer'), may hold values from -1 to 2, as said below
- pivot_inverse: bfloat16 [4, 128, 128], replicated, may hold values from -0.1 to 0.1, as said below
- pattern: int32 [16, 2, 32], P('layer'), may hold values 0 or 1
- col_order: int32 [32], replicated, may hold values from 0 to 31, each once
- sep_blocks: int32 [4], replicated, may hold values from 0 to 31, as said below
Outputs:
- schur_top: bfloat16 [4096, 4096], P('layer', 'col')
The draws below stay inside these ranges and needn't reach their ends.
Inputs may be any that keep to these rules, and one draw needn't show every extreme that they name: `diag_inverse`: each is the identity plus a full matrix of smaller entries. `pivot_inverse`: full matrices. `sep_blocks`: the 4 entries are distinct.
All inputs are finite; a program needn't handle non-finite values. No bound on the sum of `pattern` on one device may be relied on, other than what follows from the above.
Results may differ from the reference program's by a relative error of at most 0.0088.
Values may be sent and summed in bfloat16 or wider, within the bound.
No kernel may reach another device: no remote copies, remote signals or barrier semaphores. Data moves between devices by JAX's collectives and lax.ppermute only.
A program may use at most 64 MiB of HBM per device.

```python
import math
import jax
import jax.numpy as jnp
from jax import lax

S = 4096
SN = 768
NSUP = 1
NB = 128
SEP = 128
LAYERS = 16
LEVELS = 4
NBLK = 32
N_LAYER = 16


def draw_diag_inverse(key, part):
    shape = (LAYERS, NSUP, SN, SN)
    noise = 0.5 * jnp.clip(jax.random.normal(key, shape, jnp.float32), -4.0, 4.0)
    value = jnp.eye(SN, dtype=jnp.float32) + noise / math.sqrt(SN)
    return value.astype(jnp.bfloat16)


def draw_pivot_inverse(key, part):
    shape = (LEVELS, SEP, SEP)
    noise = 0.5 * jnp.clip(jax.random.normal(key, shape, jnp.float32), -4.0, 4.0)
    value = (jnp.eye(SEP, dtype=jnp.float32) + noise / math.sqrt(SEP)) / 32.0
    return value.astype(jnp.bfloat16)


def draw_sep_blocks(key, part):
    order = jax.random.permutation(jax.random.fold_in(key, 17), S // NB)
    return order[:LEVELS].astype(jnp.int32)


def place_ends(array, stream_key, least, top_value):
    spot = [jax.random.randint(jax.random.fold_in(stream_key, axis), (), 0, length) for axis, length in enumerate(array.shape)]
    longest = array.shape.index(max(array.shape))
    neighbour = spot[:longest] + [(spot[longest] + 1) % array.shape[longest]] + spot[longest + 1:]
    return array.at[tuple(spot)].set(least).at[tuple(neighbour)].set(top_value)


def level_of(own_key, shape, split, low, largest):
    factor_of, own = 1.0, jax.random.fold_in(own_key, 6)
    for axis_at, blocks in split:
        draws = jnp.exp(jax.random.uniform(jax.random.fold_in(own, axis_at), (blocks,), jnp.float32, low / len(split), largest / len(split)))
        factor_of = factor_of * jnp.repeat(draws, shape[axis_at] // blocks).reshape([-1 if axis == axis_at else 1 for axis in range(len(shape))])
    return factor_of


def gaussian(stream_key, extent, scale, most, shards=(), held_as=jnp.bfloat16):
    gain = level_of(stream_key, extent, shards, -0.22, 0.18) if shards else 1.0
    entries = jax.random.normal(stream_key, extent, jnp.float32) * scale * gain
    return jnp.minimum(jnp.maximum(entries, -most), most).astype(held_as)


def setup_inputs(seed: int = 0) -> dict:
    keys = jax.random.split(jax.random.key(seed), 8)
    lower_panel = gaussian(keys[0], (LAYERS, S, NSUP * SN), (4 * NSUP * SN) ** -0.5, 0.109375, ((0, 16), (1, 32)))
    upper_panel = gaussian(keys[1], (LAYERS, NSUP * SN, S), 1.0, 6.0, ((0, 16), (2, 32)))
    diag_inverse = draw_diag_inverse(jax.random.fold_in(keys[7], 71), 0)
    pivot_inverse = draw_pivot_inverse(jax.random.fold_in(keys[7], 71), 0)
    pattern = place_ends((jax.random.randint(keys[4], (LAYERS, 2, NBLK), 0, 2) < 1).astype(jnp.int32), jax.random.fold_in(keys[4], 1), 0, 1)
    col_order = jax.random.permutation(keys[5], NBLK).astype(jnp.int32)
    sep_blocks = draw_sep_blocks(jax.random.fold_in(keys[7], 71), 0)
    return {"lower_panel": lower_panel, "upper_panel": upper_panel, "diag_inverse": diag_inverse, "pivot_inverse": pivot_inverse, "pattern": pattern, "col_order": col_order, "sep_blocks": sep_blocks}


def layer_block(lower, upper, inverse, flags):
    width = NSUP * SN
    solved = jnp.einsum("sab,sbc->sac", inverse.astype(jnp.float32), upper.reshape(NSUP, SN, S).astype(jnp.float32))
    right = solved.reshape(width, S).astype(jnp.bfloat16)
    product = jnp.dot(lower, right, preferred_element_type=jnp.float32)
    row_flags = jnp.repeat(flags[0], NB).astype(jnp.float32)
    col_flags = jnp.repeat(flags[1], NB).astype(jnp.float32)
    return (-product * row_flags[:, None] * col_flags[None, :]).astype(jnp.bfloat16)


def eliminate(total, pivot, separator, position):
    panel = lax.dynamic_slice_in_dim(total, (position * NB).astype(jnp.int32), NB, 1).astype(jnp.bfloat16)
    factor = jnp.dot(panel, pivot, preferred_element_type=jnp.float32).astype(jnp.bfloat16)
    upper_rows = lax.dynamic_slice_in_dim(total, (separator * NB).astype(jnp.int32), NB, 0).astype(jnp.bfloat16)
    updated = total - jnp.dot(factor, upper_rows, preferred_element_type=jnp.float32)
    row_keep = (jnp.arange(S, dtype=jnp.int32) // NB) != separator
    col_keep = (jnp.arange(S, dtype=jnp.int32) // NB) != position
    kept = jnp.where(row_keep[:, None] & col_keep[None, :], updated, jnp.zeros_like(updated))
    return kept.astype(jnp.bfloat16)


def reference(lower_panel, upper_panel, diag_inverse, pivot_inverse, pattern, col_order, sep_blocks):
    blocks = []
    for layer_index in range(N_LAYER):
        blocks.append(layer_block(lower_panel[layer_index], upper_panel[layer_index], diag_inverse[layer_index], pattern[layer_index]))
    positions = jnp.arange(NBLK, dtype=jnp.int32)
    for level in range(LEVELS):
        separator = sep_blocks[level].astype(jnp.int32)
        position = jnp.sum(jnp.where(col_order == separator, positions, 0)).astype(jnp.int32)
        joined = []
        for pair_index in range(len(blocks) // 2):
            total = blocks[2 * pair_index].astype(jnp.float32) + blocks[2 * pair_index + 1].astype(jnp.float32)
            joined.append(eliminate(total, pivot_inverse[level], separator, position))
        blocks = joined
    return blocks[0]
```

```python
import jax
import jax.numpy as jnp
from jax import lax
from jax.sharding import Mesh
from jax.sharding import PartitionSpec as P

NB = 128
COL = ("zl", "y")
F32 = jnp.float32
BF16 = jnp.bfloat16


def dot(a, b):
    return jnp.dot(a, b, preferred_element_type=F32)


def swap(value, axis, mask):
    return lax.ppermute(value, axis, [(i, i ^ mask) for i in range(lax.axis_size(axis))])


def gather(value, axis):
    n = lax.axis_size(axis)
    me = lax.axis_index(axis)
    parts = [value]
    for r in range(1, n):
        parts.append(lax.ppermute(value, axis, [(i, (i + r) % n) for i in range(n)]))
    return me, parts


def ordered(me, parts):
    n = len(parts)
    stacked = jnp.zeros((n,) + parts[0].shape, parts[0].dtype)
    for r, part in enumerate(parts):
        stacked = lax.dynamic_update_index_in_dim(stacked, part, (me - r) % n, 0)
    return stacked


def shards(lower_panel, upper_panel, diag_inverse, pivot_inverse, pattern, col_order, sep_blocks):
    supernodes, node_width = diag_inverse.shape[1], diag_inverse.shape[2]
    width = supernodes * node_width
    nz, ny, nx = lax.axis_size("zl"), lax.axis_size("y"), lax.axis_size("x")
    zl, y, x = lax.axis_index("zl"), lax.axis_index("y"), lax.axis_index("x")
    zh, core = lax.axis_index("zh"), lax.axis_index("core")
    ncol = nz * ny
    me = zl * ny + y
    layer = (x * 2 + zh) * 2 + core
    levels = sep_blocks.shape[0]
    nblocks = col_order.shape[0]
    positions = jnp.arange(nblocks, dtype=jnp.int32)
    pos_blocks = jnp.sum(jnp.where(col_order[None, :] == sep_blocks[:, None], positions[None, :], 0), axis=1)

    solved = jnp.einsum(
        "sab,sbc->sac",
        diag_inverse[0],
        upper_panel[0].reshape(supernodes, node_width, NB),
        preferred_element_type=F32,
    ).reshape(width, NB)
    right = (solved * pattern[0, 1, me].astype(F32)).astype(BF16)
    left = lower_panel[0] * (-pattern[0, 0, me]).astype(BF16)

    kblocks = width // NB
    rows = width // ncol
    left_stack = left.reshape(NB, kblocks, NB).transpose(1, 0, 2).reshape(ncol, rows, NB)
    send = jnp.stack([left_stack, right.reshape(ncol, rows, NB)], axis=1)
    got = lax.all_to_all(send, COL, 0, 0, tiled=True)
    picked = [lax.dynamic_index_in_dim(got[:, 0], sep_blocks[k], 0) for k in range(levels)]
    picked += [lax.dynamic_index_in_dim(got[:, 1], pos_blocks[k], 0) for k in range(levels)]
    picked = jnp.concatenate(picked, 0)
    spread = lax.all_to_all(jnp.broadcast_to(picked[None], (ncol,) + picked.shape), COL, 0, 0, tiled=True)
    spread = spread.transpose(1, 0, 2, 3).reshape(2 * levels, width, NB)
    left_sep = spread[:levels].reshape(levels, kblocks, NB, NB).transpose(0, 2, 1, 3).reshape(levels * NB, width)
    right_pos = [spread[levels + k] for k in range(levels)]

    tile_me, tile_parts = gather(right, "zl")
    right_tile = jnp.concatenate(list(ordered(tile_me, tile_parts)), axis=1)
    left_me, left_parts = gather(left, "y")
    left_tile = ordered(left_me, left_parts).reshape(ny * NB, width)

    state = dot(left_sep, jnp.concatenate(right_pos + [right_tile], axis=1)).astype(BF16)
    panels, fills = [], []
    axes = (("core", 1), ("zh", 1), ("x", 1), ("x", 2))
    for k in range(levels):
        if k == levels - 1:
            state = state[:, NB:]
        axis, mask = axes[k]
        total = state.astype(F32) + swap(state, axis, mask).astype(F32)
        skip = NB if k < levels - 1 else 0
        upper = total[:NB, skip:].astype(BF16)
        fill = dot(pivot_inverse[k], upper).astype(BF16)
        if k < levels - 1:
            panel = total[NB:, :NB].astype(BF16)
            state = (total[NB:, NB:] - dot(panel, fill)).astype(BF16)
        fills.append(fill)
        own = right_pos[k]
        if k:
            before = jnp.concatenate([fills[m][:, (k - m - 1) * NB : (k - m) * NB] for m in range(k)], axis=0)
            own = (own.astype(F32) - dot(jnp.concatenate(panels, axis=1), before)).astype(BF16)
        panels.append(own)
    tile_fill = jnp.concatenate([f[:, -nz * NB :] for f in fills], axis=0)
    right_new = (right_tile.astype(F32) - dot(jnp.concatenate(panels, axis=1), tile_fill)).astype(BF16)

    tile = dot(left_tile, right_new)
    span = 2 * NB
    tile = tile.reshape(2, 2, span, nz * NB)
    keep = lax.dynamic_index_in_dim(tile, core, 1, keepdims=False)
    give = lax.dynamic_index_in_dim(tile, 1 - core, 1, keepdims=False).astype(BF16)
    half = keep + swap(give, "core", 1).astype(F32)
    pieces = half.astype(BF16).reshape(2 * span, nz, NB).transpose(1, 0, 2)
    summed = jnp.zeros((2 * span, NB), F32)
    for r in range(nx):
        piece = lax.dynamic_index_in_dim(pieces, (x + r) % nx, 0, keepdims=False)
        pairs = [(a * nz + b, b * nz + (a + r) % nx) for a in range(nx) for b in range(nz)]
        summed = summed + lax.ppermute(piece, ("x", "zl"), pairs).astype(F32)
    summed = summed.reshape(2, span, NB)
    keep = lax.dynamic_index_in_dim(summed, zh, 0, keepdims=False)
    give = lax.dynamic_index_in_dim(summed, 1 - zh, 0, keepdims=False).astype(BF16)
    out = keep + swap(give, "zh", 1).astype(F32)
    row_blocks = layer * 2 + jnp.arange(span, dtype=jnp.int32) // NB
    row_keep = jnp.all(row_blocks[:, None] != sep_blocks[None, :], axis=1)
    col_keep = jnp.all(pos_blocks != me)
    return jnp.where(row_keep[:, None] & col_keep, out, 0.0).astype(BF16)


def solution(mesh):
    fine = Mesh(mesh.devices.reshape(4, 2, 2, 4, 8), ("x", "zh", "core", "zl", "y"))
    lay = ("x", "zh", "core")
    in_specs = (
        P(lay, COL, None),
        P(lay, None, COL),
        P(lay, None, None, None),
        P(),
        P(lay, None, None),
        P(),
        P(),
    )
    return jax.shard_map(shards, mesh=fine, in_specs=in_specs, out_specs=P(lay, COL), check_vma=False)
```

```python
import jax
import jax.numpy as jnp
from jax import lax
from jax.experimental import pallas as pl
from jax.experimental.pallas import tpu as pltpu
from jax.sharding import Mesh
from jax.sharding import PartitionSpec as P

NB = 128
COL = ("zl", "y")
F32 = jnp.float32
BF16 = jnp.bfloat16


def dot(a, b):
    return jnp.dot(a, b, preferred_element_type=F32)


def swap(value, axis, mask):
    return lax.ppermute(value, axis, [(i, i ^ mask) for i in range(lax.axis_size(axis))])


def spread(value, axis, n):
    return lax.all_to_all(jnp.broadcast_to(value[None], (n,) + value.shape), axis, 0, 0, tiled=True)


VMEM = pl.BlockSpec(memory_space=pltpu.VMEM)
SMEM = pl.BlockSpec(memory_space=pltpu.SMEM)


def solve_into(diag_ref, upper, scale, out_ref, columns):
    supernodes, node = diag_ref.shape[0], diag_ref.shape[1]
    for s in range(supernodes):
        here = pl.ds(s * node, node)
        solved = dot(diag_ref[s], upper[s * node : (s + 1) * node])
        out_ref[here, columns] = (solved * scale).astype(BF16)


def sep_kernel(col_ref, row_ref, parts_ref, diag_ref, upper_ref, pos_ref, own_ref, state_ref, left_ref):
    levels = row_ref.shape[0]
    wide = levels * NB
    lane = lax.broadcasted_iota(jnp.int32, (1, 2 * NB), 1)
    solve_into(diag_ref, upper_ref[...], col_ref[levels], own_ref, pl.ds(0, NB))
    for k in range(0, levels, 2):
        upper = jnp.concatenate([parts_ref[levels + k], parts_ref[levels + k + 1]], axis=1)
        scale = jnp.where(lane < NB, col_ref[k], col_ref[k + 1])
        solve_into(diag_ref, upper, scale, pos_ref, pl.ds(k * NB, 2 * NB))
    for k in range(levels):
        for j in range(left_ref.shape[1] // NB):
            left_ref[k * NB : (k + 1) * NB, j * NB : (j + 1) * NB] = parts_ref[k, j * NB : (j + 1) * NB, :]
    low = lax.broadcasted_iota(jnp.int32, (wide, 1), 0) // NB
    sign = jnp.zeros((wide, 1), F32)
    for k in range(levels):
        sign = jnp.where(low == k, -row_ref[k], sign)
    state_ref[:, :wide] = (dot(left_ref[...], pos_ref[...]) * sign).astype(BF16)
    state_ref[:, wide:] = (dot(left_ref[...], own_ref[...]) * sign).astype(BF16)


def product_kernel(pick_ref, flag_ref, left_ref, *refs):
    out_ref, right_ref = refs[-2:]
    for r, part in enumerate(refs[:-2]):
        right_ref[r] = part[...]
    right = jnp.concatenate([right_ref[pick_ref[0]], right_ref[pick_ref[1]]], axis=1)
    for q in range(left_ref.shape[0]):
        here = pl.ds(q * NB, NB)
        out_ref[here, :] = (dot(left_ref[q], right) * flag_ref[q]).astype(out_ref.dtype)


def call(kernel, outs, specs, scratch=(), dtype=BF16):
    return pl.pallas_call(
        kernel,
        out_shape=[jax.ShapeDtypeStruct(o, dtype) for o in outs],
        in_specs=specs,
        out_specs=[VMEM] * len(outs),
        scratch_shapes=list(scratch),
        compiler_params=pltpu.CompilerParams(vmem_limit_bytes=40 * 2**20),
    )


def shards(lower_panel, upper_panel, diag_inverse, pivot_inverse, pattern, col_order, sep_blocks):
    width = diag_inverse.shape[1] * diag_inverse.shape[2]
    nz, ny = lax.axis_size("zl"), lax.axis_size("y")
    zl, y, x = lax.axis_index("zl"), lax.axis_index("y"), lax.axis_index("x")
    zh, core = lax.axis_index("zh"), lax.axis_index("core")
    ncol = nz * ny
    me = zl * ny + y
    layer = (x * 2 + zh) * 2 + core
    levels = sep_blocks.shape[0]
    nblocks = col_order.shape[0]
    positions = jnp.arange(nblocks, dtype=jnp.int32)
    pos_blocks = jnp.sum(jnp.where(col_order[None, :] == sep_blocks[:, None], positions[None, :], 0), axis=1)
    row_flags, col_flags = pattern[0, 0].astype(F32), pattern[0, 1].astype(F32)
    left, upper_own = lower_panel[0], upper_panel[0]

    kblocks = width // NB
    rows = width // ncol
    left_stack = left.reshape(NB, kblocks, NB).transpose(1, 0, 2).reshape(ncol, rows, NB)
    send = jnp.stack([left_stack, upper_own.reshape(ncol, rows, NB)], axis=1)
    got = lax.all_to_all(send, COL, 0, 0, tiled=True)
    picked = [lax.dynamic_index_in_dim(got[:, 0], sep_blocks[k], 0) for k in range(levels)]
    picked += [lax.dynamic_index_in_dim(got[:, 1], pos_blocks[k], 0) for k in range(levels)]
    picked = jnp.concatenate(picked, 0)
    picked, left_late = lax.optimization_barrier((picked, left))
    parts = spread(picked, COL, ncol).transpose(1, 0, 2, 3).reshape(2 * levels, width, NB)
    left_moved = lax.ppermute(
        left_late, COL, [(a * ny + b, (b // 2) * ny + 2 * a + b % 2) for a in range(nz) for b in range(ny)]
    )

    pos_width, half = levels * NB, nz * NB // 2
    flags = jnp.concatenate([col_flags[pos_blocks], col_flags[me][None]])
    right_pos, right_own, state = call(
        sep_kernel,
        [(width, pos_width), (width, NB), (pos_width, pos_width + NB)],
        [SMEM] * 2 + [VMEM] * 3,
        [pltpu.VMEM((pos_width, width), BF16)],
    )(flags, row_flags[sep_blocks], parts, diag_inverse[0], upper_own)

    state, left_moved = lax.optimization_barrier((state, left_moved))
    left_tile = spread(left_moved, "y", ny)
    panels, fills = [], []
    axes = (("core", 1), ("zh", 1), ("x", 1), ("x", 2))
    for k in range(levels):
        if k == levels - 1:
            state = state[:, NB:]
        axis, mask = axes[k]
        other = swap(state, axis, mask)
        total = state.astype(F32) + other.astype(F32)
        skip = NB if k < levels - 1 else 0
        fill = dot(pivot_inverse[k], total[:NB, skip:].astype(BF16)).astype(BF16)
        if k < levels - 1:
            panel = total[NB:, :NB].astype(BF16)
            state = (total[NB:, NB:] - dot(panel, fill)).astype(BF16)
        fills.append(fill)
        own = right_pos[:, k * NB : (k + 1) * NB]
        if k:
            before = jnp.concatenate([fills[m][:, (k - m - 1) * NB : (k - m) * NB] for m in range(k)], axis=0)
            own = (own.astype(F32) - dot(jnp.concatenate(panels, axis=1), before)).astype(BF16)
        panels.append(own)
    fill_own = jnp.concatenate([f[:, -NB:] for f in fills], axis=0)
    right_new = (right_own.astype(F32) - dot(jnp.concatenate(panels, axis=1), fill_own)).astype(BF16)
    right_parts = [right_new] + [
        lax.ppermute(right_new, "zl", [(i, (i + r) % nz) for i in range(nz)]) for r in range(1, nz)
    ]

    tile_rows = jnp.arange(nz, dtype=jnp.int32)[:, None] * 8 + 2 * zl + jnp.arange(2, dtype=jnp.int32)[None, :]
    tile_flags = -row_flags[tile_rows.reshape(-1)]

    def product(which, dtype):
        picks = (zl - 2 * which - jnp.arange(2, dtype=jnp.int32)) % nz
        specs = [SMEM] * 2 + [VMEM] * (1 + nz)
        scratch = [pltpu.VMEM((nz, width, NB), BF16)]
        return call(product_kernel, [(ny * NB, half)], specs, scratch, dtype)(picks, tile_flags, left_tile, *right_parts)[0]

    taken = swap(product(1 - core, BF16), "core", 1)
    both = (product(core, F32) + taken.astype(F32)).astype(BF16).reshape(nz, 2 * NB, half)
    summed = jnp.sum(lax.all_to_all(both, "x", 0, 0, tiled=True).astype(F32), axis=0)
    pairs = [
        [((a * 2 + b) * nz + c, c * nz + 2 * b + (r ^ a)) for a in range(2) for b in range(2) for c in range(nz)]
        for r in range(2)
    ]
    summed = summed.astype(BF16)
    first = lax.dynamic_slice_in_dim(summed, zh * NB, NB, 1)
    second = lax.dynamic_slice_in_dim(summed, (1 - zh) * NB, NB, 1)
    first = lax.ppermute(first, ("zh", "core", "zl"), pairs[0])
    second = lax.ppermute(second, ("zh", "core", "zl"), pairs[1])
    out = first.astype(F32) + second.astype(F32)
    row_blocks = layer * 2 + jnp.arange(2 * NB, dtype=jnp.int32) // NB
    row_keep = jnp.all(row_blocks[:, None] != sep_blocks[None, :], axis=1)
    col_keep = jnp.all(pos_blocks != me)
    return jnp.where(row_keep[:, None] & col_keep, out, 0.0).astype(BF16)


def solution(mesh):
    fine = Mesh(mesh.devices.reshape(4, 2, 2, 4, 8), ("x", "zh", "core", "zl", "y"))
    lay = ("x", "zh", "core")
    in_specs = (
        P(lay, COL, None),
        P(lay, None, COL),
        P(lay, None, None, None),
        P(),
        P(lay, None, None),
        P(),
        P(),
    )
    return jax.shard_map(shards, mesh=fine, in_specs=in_specs, out_specs=P(lay, COL), check_vma=False)
```

```python
import jax
import jax.numpy as jnp
from jax import lax
from jax.experimental import pallas as pl
from jax.experimental.pallas import tpu as pltpu
from jax.sharding import Mesh
from jax.sharding import PartitionSpec as P

NB = 128
COL = ("zl", "y")
F32 = jnp.float32
BF16 = jnp.bfloat16


def dot(a, b):
    return jnp.dot(a, b, preferred_element_type=F32)


def swap(value, axis, mask):
    return lax.ppermute(value, axis, [(i, i ^ mask) for i in range(lax.axis_size(axis))])


def exchange(value, nz, ny):
    n = nz * ny
    groups = [list(range(n)), list(range(2 * n - 1, n - 1, -1))]
    return lax.all_to_all(value, ("core",) + COL, 0, 0, axis_index_groups=groups, tiled=True)


def spread(value, n, nz, ny):
    return exchange(jnp.broadcast_to(value[None], (n,) + value.shape), nz, ny)


VMEM = pl.BlockSpec(memory_space=pltpu.VMEM)
SMEM = pl.BlockSpec(memory_space=pltpu.SMEM)


def solve_into(diag_ref, upper, scale, out_ref, columns):
    supernodes, node = diag_ref.shape[0], diag_ref.shape[1]
    for s in range(supernodes):
        here = pl.ds(s * node, node)
        solved = dot(diag_ref[s], upper[s * node : (s + 1) * node])
        out_ref[here, columns] = (solved * scale).astype(BF16)


def sep_kernel(col_ref, row_ref, parts_ref, diag_ref, upper_ref, pos_ref, own_ref, state_ref, left_ref):
    levels = row_ref.shape[0]
    wide = levels * NB
    lane = lax.broadcasted_iota(jnp.int32, (1, 2 * NB), 1)
    solve_into(diag_ref, upper_ref[...], col_ref[levels], own_ref, pl.ds(0, NB))
    for k in range(0, levels, 2):
        upper = jnp.concatenate([parts_ref[levels + k], parts_ref[levels + k + 1]], axis=1)
        scale = jnp.where(lane < NB, col_ref[k], col_ref[k + 1])
        solve_into(diag_ref, upper, scale, pos_ref, pl.ds(k * NB, 2 * NB))
    for k in range(levels):
        for j in range(left_ref.shape[1] // NB):
            left_ref[k * NB : (k + 1) * NB, j * NB : (j + 1) * NB] = parts_ref[k, j * NB : (j + 1) * NB, :]
    low = lax.broadcasted_iota(jnp.int32, (wide, 1), 0) // NB
    sign = jnp.zeros((wide, 1), F32)
    for k in range(levels):
        sign = jnp.where(low == k, -row_ref[k], sign)
    state_ref[:, :wide] = (dot(left_ref[...], pos_ref[...]) * sign).astype(BF16)
    state_ref[:, wide:] = (dot(left_ref[...], own_ref[...]) * sign).astype(BF16)


def product_kernel(pick_ref, flag_ref, left_ref, *refs):
    out_ref, right_ref = refs[-2:]
    for r, part in enumerate(refs[:-2]):
        right_ref[r] = part[...]
    right = jnp.concatenate([right_ref[pick_ref[0]], right_ref[pick_ref[1]]], axis=1)
    for q in range(left_ref.shape[0]):
        here = pl.ds(q * NB, NB)
        out_ref[here, :] = (dot(left_ref[q], right) * flag_ref[q]).astype(out_ref.dtype)


def call(kernel, outs, specs, scratch=(), dtype=BF16):
    return pl.pallas_call(
        kernel,
        out_shape=[jax.ShapeDtypeStruct(o, dtype) for o in outs],
        in_specs=specs,
        out_specs=[VMEM] * len(outs),
        scratch_shapes=list(scratch),
        compiler_params=pltpu.CompilerParams(vmem_limit_bytes=40 * 2**20),
    )


def shards(lower_panel, upper_panel, diag_inverse, pivot_inverse, pattern, col_order, sep_blocks):
    width = diag_inverse.shape[1] * diag_inverse.shape[2]
    nz, ny = lax.axis_size("zl"), lax.axis_size("y")
    zl, y, x = lax.axis_index("zl"), lax.axis_index("y"), lax.axis_index("x")
    zh, core = lax.axis_index("zh"), lax.axis_index("core")
    ncol = nz * ny
    me = zl * ny + y
    layer = (x * 2 + zh) * 2 + core
    levels = sep_blocks.shape[0]
    nblocks = col_order.shape[0]
    positions = jnp.arange(nblocks, dtype=jnp.int32)
    pos_blocks = jnp.sum(jnp.where(col_order[None, :] == sep_blocks[:, None], positions[None, :], 0), axis=1)
    row_flags, col_flags = pattern[0, 0].astype(F32), pattern[0, 1].astype(F32)
    left, upper_own = lower_panel[0], upper_panel[0]

    kblocks = width // NB
    rows = width // ncol
    left_stack = left.reshape(NB, kblocks, NB).transpose(1, 0, 2).reshape(ncol, rows, NB)
    send = jnp.stack([left_stack, upper_own.reshape(ncol, rows, NB)], axis=1)
    got = exchange(send, nz, ny)

    def place(member):
        return jnp.where(core == 1, ncol - 1 - member, member)

    picked = [lax.dynamic_index_in_dim(got[:, 0], place(sep_blocks[k]), 0) for k in range(levels)]
    picked += [lax.dynamic_index_in_dim(got[:, 1], place(pos_blocks[k]), 0) for k in range(levels)]
    picked = jnp.concatenate(picked, 0)
    picked, left_late = lax.optimization_barrier((picked, left))
    parts = spread(picked, ncol, nz, ny).transpose(1, 0, 2, 3).reshape(2 * levels, width, NB)
    left_moved = lax.ppermute(
        left_late, COL, [(a * ny + b, (b // 2) * ny + 2 * a + b % 2) for a in range(nz) for b in range(ny)]
    )

    pos_width, half = levels * NB, nz * NB // 2
    flags = jnp.concatenate([col_flags[pos_blocks], col_flags[me][None]])
    right_pos, right_own, state = call(
        sep_kernel,
        [(width, pos_width), (width, NB), (pos_width, pos_width + NB)],
        [SMEM] * 2 + [VMEM] * 3,
        [pltpu.VMEM((pos_width, width), BF16)],
    )(flags, row_flags[sep_blocks], parts, diag_inverse[0], upper_own)

    state, left_moved = lax.optimization_barrier((state, left_moved))
    copies = jnp.broadcast_to(left_moved[None], (ny,) + left_moved.shape)
    left_tile = lax.all_to_all(copies, "y", 0, 0, tiled=True)
    panels, fills = [], []
    axes = (("core", 1), ("zh", 1), ("x", 1), ("x", 2))
    for k in range(levels):
        if k == levels - 1:
            state = state[:, NB:]
        axis, mask = axes[k]
        if axis == "zh":
            part = state.shape[0] // 2
            crossed = swap(lax.dynamic_slice_in_dim(state, core * part, part, 0), axis, mask)
        else:
            other = swap(state, axis, mask)
        if axis == "zh":
            shared = swap(crossed, "core", 1)
            first = core == 0
            other = jnp.concatenate([jnp.where(first, crossed, shared), jnp.where(first, shared, crossed)], axis=0)
        total = state.astype(F32) + other.astype(F32)
        skip = NB if k < levels - 1 else 0
        fill = dot(pivot_inverse[k], total[:NB, skip:].astype(BF16)).astype(BF16)
        if k < levels - 1:
            panel = total[NB:, :NB].astype(BF16)
            state = (total[NB:, NB:] - dot(panel, fill)).astype(BF16)
        fills.append(fill)
        own = right_pos[:, k * NB : (k + 1) * NB]
        if k:
            before = jnp.concatenate([fills[m][:, (k - m - 1) * NB : (k - m) * NB] for m in range(k)], axis=0)
            own = (own.astype(F32) - dot(jnp.concatenate(panels, axis=1), before)).astype(BF16)
        panels.append(own)
    fill_own = jnp.concatenate([f[:, -NB:] for f in fills], axis=0)
    right_new = (right_own.astype(F32) - dot(jnp.concatenate(panels, axis=1), fill_own)).astype(BF16)
    right_parts = [right_new] + [
        swap(right_new, "zl", r) for r in range(1, nz)
    ]

    tile_rows = jnp.arange(nz, dtype=jnp.int32)[:, None] * 8 + 2 * zl + jnp.arange(2, dtype=jnp.int32)[None, :]
    tile_flags = -row_flags[tile_rows.reshape(-1)]

    def product(which, dtype):
        picks = zl ^ (2 * which + jnp.arange(2, dtype=jnp.int32))
        specs = [SMEM] * 2 + [VMEM] * (1 + nz)
        scratch = [pltpu.VMEM((nz, width, NB), BF16)]
        return call(product_kernel, [(ny * NB, half)], specs, scratch, dtype)(picks, tile_flags, left_tile, *right_parts)[0]

    taken = swap(product(1 - core, BF16), "core", 1)
    both = (product(core, F32) + taken.astype(F32)).astype(BF16).reshape(nz, 2 * NB, half)
    summed = jnp.sum(lax.all_to_all(both, "x", 0, 0, tiled=True).astype(F32), axis=0)
    pairs = [
        [((a * 2 + b) * nz + c, c * nz + 2 * b + (r ^ a)) for a in range(2) for b in range(2) for c in range(nz)]
        for r in range(2)
    ]
    summed = summed.astype(BF16)
    first = lax.dynamic_slice_in_dim(summed, zh * NB, NB, 1)
    second = lax.dynamic_slice_in_dim(summed, (1 - zh) * NB, NB, 1)
    first = lax.ppermute(first, ("zh", "core", "zl"), pairs[0])
    second = lax.ppermute(second, ("zh", "core", "zl"), pairs[1])
    out = first.astype(F32) + second.astype(F32)
    row_blocks = layer * 2 + jnp.arange(2 * NB, dtype=jnp.int32) // NB
    row_keep = jnp.all(row_blocks[:, None] != sep_blocks[None, :], axis=1)
    col_keep = jnp.all(pos_blocks != me)
    return jnp.where(row_keep[:, None] & col_keep, out, 0.0).astype(BF16)


def solution(mesh):
    fine = Mesh(mesh.devices.reshape(4, 2, 2, 4, 8), ("x", "zh", "core", "zl", "y"))
    lay = ("x", "zh", "core")
    in_specs = (
        P(lay, COL, None),
        P(lay, None, COL),
        P(lay, None, None, None),
        P(),
        P(lay, None, None),
        P(),
        P(),
    )
    return jax.shard_map(shards, mesh=fine, in_specs=in_specs, out_specs=P(lay, COL), check_vma=False)
```

```python
import jax
import jax.numpy as jnp
from jax import lax
from jax.experimental import pallas as pl
from jax.experimental.pallas import tpu as pltpu
from jax.sharding import Mesh
from jax.sharding import PartitionSpec as P

NB = 128
COL = ("zl", "y")
F32 = jnp.float32
BF16 = jnp.bfloat16


def dot(a, b):
    return jnp.dot(a, b, preferred_element_type=F32)


def swap(value, axis, mask):
    return lax.ppermute(value, axis, [(i, i ^ mask) for i in range(lax.axis_size(axis))])


def exchange(value, nz, ny):
    n = nz * ny
    groups = [list(range(n)), list(range(2 * n - 1, n - 1, -1))]
    return lax.all_to_all(value, ("core",) + COL, 0, 0, axis_index_groups=groups, tiled=True)


def spread(value, n, nz, ny):
    return exchange(jnp.broadcast_to(value[None], (n,) + value.shape), nz, ny)


VMEM = pl.BlockSpec(memory_space=pltpu.VMEM)
SMEM = pl.BlockSpec(memory_space=pltpu.SMEM)


def solve_into(diag_ref, upper, scale, out_ref, columns):
    supernodes, node = diag_ref.shape[0], diag_ref.shape[1]
    for s in range(supernodes):
        here = pl.ds(s * node, node)
        solved = dot(diag_ref[s], upper[s * node : (s + 1) * node])
        out_ref[here, columns] = (solved * scale).astype(BF16)


def sep_kernel(col_ref, row_ref, parts_ref, diag_ref, upper_ref, pos_ref, own_ref, state_ref, left_ref):
    levels = row_ref.shape[0]
    wide = levels * NB
    lane = lax.broadcasted_iota(jnp.int32, (1, 2 * NB), 1)
    solve_into(diag_ref, upper_ref[...], col_ref[levels], own_ref, pl.ds(0, NB))
    for k in range(0, levels, 2):
        upper = jnp.concatenate([parts_ref[levels + k], parts_ref[levels + k + 1]], axis=1)
        scale = jnp.where(lane < NB, col_ref[k], col_ref[k + 1])
        solve_into(diag_ref, upper, scale, pos_ref, pl.ds(k * NB, 2 * NB))
    for k in range(levels):
        for j in range(left_ref.shape[1] // NB):
            left_ref[k * NB : (k + 1) * NB, j * NB : (j + 1) * NB] = parts_ref[k, j * NB : (j + 1) * NB, :]
    low = lax.broadcasted_iota(jnp.int32, (wide, 1), 0) // NB
    sign = jnp.zeros((wide, 1), F32)
    for k in range(levels):
        sign = jnp.where(low == k, -row_ref[k], sign)
    state_ref[:, :wide] = (dot(left_ref[...], pos_ref[...]) * sign).astype(BF16)
    state_ref[:, wide:] = (dot(left_ref[...], own_ref[...]) * sign).astype(BF16)


def product_kernel(pick_ref, flag_ref, left_ref, *refs):
    out_ref, right_ref = refs[-2:]
    for r, part in enumerate(refs[:-2]):
        right_ref[r] = part[...]
    right = jnp.concatenate([right_ref[pick_ref[0]], right_ref[pick_ref[1]]], axis=1)
    for q in range(left_ref.shape[0]):
        here = pl.ds(pl.multiple_of(pick_ref[2 + q] * NB, NB), NB)
        out_ref[here, :] = (dot(left_ref[q], right) * flag_ref[q]).astype(out_ref.dtype)


def call(kernel, outs, specs, scratch=(), dtype=BF16):
    return pl.pallas_call(
        kernel,
        out_shape=[jax.ShapeDtypeStruct(o, dtype) for o in outs],
        in_specs=specs,
        out_specs=[VMEM] * len(outs),
        scratch_shapes=list(scratch),
        compiler_params=pltpu.CompilerParams(vmem_limit_bytes=40 * 2**20),
    )


def shards(lower_panel, upper_panel, diag_inverse, pivot_inverse, pattern, col_order, sep_blocks):
    width = diag_inverse.shape[1] * diag_inverse.shape[2]
    nz, ny = lax.axis_size("zl"), lax.axis_size("y")
    zl, y, x = lax.axis_index("zl"), lax.axis_index("y"), lax.axis_index("x")
    zh, core = lax.axis_index("zh"), lax.axis_index("core")
    ncol = nz * ny
    me = zl * ny + y
    layer = (x * 2 + zh) * 2 + core
    levels = sep_blocks.shape[0]
    nblocks = col_order.shape[0]
    positions = jnp.arange(nblocks, dtype=jnp.int32)
    pos_blocks = jnp.sum(jnp.where(col_order[None, :] == sep_blocks[:, None], positions[None, :], 0), axis=1)
    row_flags, col_flags = pattern[0, 0].astype(F32), pattern[0, 1].astype(F32)
    left, upper_own = lower_panel[0], upper_panel[0]

    kblocks = width // NB
    rows = width // ncol
    left_stack = left.reshape(NB, kblocks, NB).transpose(1, 0, 2).reshape(ncol, rows, NB)
    send = jnp.stack([left_stack, upper_own.reshape(ncol, rows, NB)], axis=1)
    got = exchange(send, nz, ny)

    def place(member):
        return jnp.where(core == 1, ncol - 1 - member, member)

    picked = [lax.dynamic_index_in_dim(got[:, 0], place(sep_blocks[k]), 0) for k in range(levels)]
    picked += [lax.dynamic_index_in_dim(got[:, 1], place(pos_blocks[k]), 0) for k in range(levels)]
    picked = jnp.concatenate(picked, 0)
    picked, left_late = lax.optimization_barrier((picked, left))
    parts = spread(picked, ncol, nz, ny).transpose(1, 0, 2, 3).reshape(2 * levels, width, NB)
    left_moved = lax.ppermute(
        left_late, COL, [(a * ny + b, (b // 2) * ny + 2 * a + b % 2) for a in range(nz) for b in range(ny)]
    )

    pos_width, half = levels * NB, nz * NB // 2
    flags = jnp.concatenate([col_flags[pos_blocks], col_flags[me][None]])
    right_pos, right_own, state = call(
        sep_kernel,
        [(width, pos_width), (width, NB), (pos_width, pos_width + NB)],
        [SMEM] * 2 + [VMEM] * 3,
        [pltpu.VMEM((pos_width, width), BF16)],
    )(flags, row_flags[sep_blocks], parts, diag_inverse[0], upper_own)

    state, left_moved = lax.optimization_barrier((state, left_moved))
    copies = jnp.broadcast_to(left_moved[None], (ny,) + left_moved.shape)
    members = [
        [(c * nz + a) * ny + (b if c == 0 else ny - 1 - b) for b in range(ny)] for c in range(2) for a in range(nz)
    ]
    left_tile = lax.all_to_all(copies, ("core",) + COL, 0, 0, axis_index_groups=members, tiled=True)
    panels, fills = [], []
    axes = (("core", 1), ("zh", 1), ("x", 1), ("x", 2))
    for k in range(levels):
        if k == levels - 1:
            state = state[:, NB:]
        axis, mask = axes[k]
        if axis == "zh":
            part = state.shape[0] // 2
            crossed = swap(lax.dynamic_slice_in_dim(state, core * part, part, 0), axis, mask)
        else:
            other = swap(state, axis, mask)
        if axis == "zh":
            shared = swap(crossed, "core", 1)
            first = core == 0
            other = jnp.concatenate([jnp.where(first, crossed, shared), jnp.where(first, shared, crossed)], axis=0)
        total = state.astype(F32) + other.astype(F32)
        skip = NB if k < levels - 1 else 0
        fill = dot(pivot_inverse[k], total[:NB, skip:].astype(BF16)).astype(BF16)
        if k < levels - 1:
            panel = total[NB:, :NB].astype(BF16)
            state = (total[NB:, NB:] - dot(panel, fill)).astype(BF16)
        fills.append(fill)
        own = right_pos[:, k * NB : (k + 1) * NB]
        if k:
            before = jnp.concatenate([fills[m][:, (k - m - 1) * NB : (k - m) * NB] for m in range(k)], axis=0)
            own = (own.astype(F32) - dot(jnp.concatenate(panels, axis=1), before)).astype(BF16)
        panels.append(own)
    fill_own = jnp.concatenate([f[:, -NB:] for f in fills], axis=0)
    right_new = (right_own.astype(F32) - dot(jnp.concatenate(panels, axis=1), fill_own)).astype(BF16)
    right_parts = [right_new] + [
        swap(right_new, "zl", r) for r in range(1, nz)
    ]

    tile_rows = jnp.arange(nz, dtype=jnp.int32)[:, None] * 8 + 2 * zl + jnp.arange(2, dtype=jnp.int32)[None, :]
    order = jnp.arange(ny, dtype=jnp.int32)
    order = jnp.where(core == 1, ny - 1 - order, order)
    tile_flags = -row_flags[tile_rows.reshape(-1)[order]]

    def product(which, dtype):
        picks = zl ^ (2 * which + jnp.arange(2, dtype=jnp.int32))
        picks = jnp.concatenate([picks, order])
        specs = [SMEM] * 2 + [VMEM] * (1 + nz)
        scratch = [pltpu.VMEM((nz, width, NB), BF16)]
        return call(product_kernel, [(ny * NB, half)], specs, scratch, dtype)(picks, tile_flags, left_tile, *right_parts)[0]

    taken = swap(product(1 - core, BF16), "core", 1)
    both = (product(core, F32) + taken.astype(F32)).astype(BF16).reshape(nz, 2 * NB, half)
    summed = jnp.sum(lax.all_to_all(both, "x", 0, 0, tiled=True).astype(F32), axis=0)
    pairs = [
        [((a * 2 + b) * nz + c, c * nz + 2 * b + (r ^ a)) for a in range(2) for b in range(2) for c in range(nz)]
        for r in range(2)
    ]
    summed = summed.astype(BF16)
    first = lax.dynamic_slice_in_dim(summed, zh * NB, NB, 1)
    second = lax.dynamic_slice_in_dim(summed, (1 - zh) * NB, NB, 1)
    first = lax.ppermute(first, ("zh", "core", "zl"), pairs[0])
    second = lax.ppermute(second, ("zh", "core", "zl"), pairs[1])
    out = first.astype(F32) + second.astype(F32)
    row_blocks = layer * 2 + jnp.arange(2 * NB, dtype=jnp.int32) // NB
    row_keep = jnp.all(row_blocks[:, None] != sep_blocks[None, :], axis=1)
    col_keep = jnp.all(pos_blocks != me)
    return jnp.where(row_keep[:, None] & col_keep, out, 0.0).astype(BF16)


def solution(mesh):
    fine = Mesh(mesh.devices.reshape(4, 2, 2, 4, 8), ("x", "zh", "core", "zl", "y"))
    lay = ("x", "zh", "core")
    in_specs = (
        P(lay, COL, None),
        P(lay, None, COL),
        P(lay, None, None, None),
        P(),
        P(lay, None, None),
        P(),
        P(),
    )
    return jax.shard_map(shards, mesh=fine, in_specs=in_specs, out_specs=P(lay, COL), check_vma=False)
```
